32 devices in a mesh: grp: 2 (over y), mesh: 16 (over z, x, core).
Axes of the slice: x: 2, y: 2, z: 4, core: 2. Of those that a mesh axis runs over, the one named last changes fastest.
Arguments:
- basis: bfloat16 [65536, 512], P(('grp', 'mesh')), parts along dimension 0, may hold values from -6 to 6
- blocks: bfloat16 [2, 512, 3, 128, 128], P(None, ('grp', 'mesh')), parts along dimension 1, may hold values from -0.0017089844 to 0.0017089844
- columns: int32 [2, 512, 2], P(None, ('grp', 'mesh')), parts along dimension 1, may hold values from 0 to 31
- sends: int32 [32, 16], P(('grp', 'mesh')), parts along dimension 0, may hold values from 0 to 15
Outputs:
- projected: float32 [1024, 1024], P(('grp', 'mesh')), parts along dimension 0
The draws below stay inside these ranges and needn't reach their ends.
There are 2 independent parts, one for each index of `grp`. The reference program is written for one: setup_inputs(seed, part) draws one part's arguments, and reference() takes and returns one part's arrays. A program takes and returns all parts, laid end to end along the dimension named above; each array names one. Nothing has to cross between parts.
All inputs are finite; a program needn't handle non-finite values.
Results may differ from the reference program's by a relative error of at most 0.0029.
Values may be sent and summed in bfloat16 or wider, within the bound.
A program may use at most 64 MiB of HBM per device.

```python
import jax
import jax.numpy as jnp
from jax import lax

BLOCK = 128
BASIS = 512
PARAMS = 2
ROWBLK = 16
SLOTS = 3
HALO = 8
NROWB = 256
NROWS = 32768
N_MESH = 16


def plant(values, own_key, smallest, largest):
    place = [jax.random.randint(jax.random.fold_in(own_key, axis), (), 0, length) for axis, length in enumerate(values.shape)]
    main_axis = values.shape.index(max(values.shape))
    beside = place[:main_axis] + [(place[main_axis] + 1) % values.shape[main_axis]] + place[main_axis + 1:]
    return values.at[tuple(place)].set(smallest).at[tuple(beside)].set(largest)


def with_spikes(drawn, key, source, target, blocks, factor):
    owner, partner = [(jnp.arange(drawn.shape[position]) // (drawn.shape[position] // blocks)).reshape([-1 if axis == position else 1 for axis in range(drawn.ndim)]) for position in (source, target)]
    chosen = jax.random.permutation(key, blocks)[partner]
    strong = (owner == chosen) | (owner == (partner + blocks // 2) % blocks)
    return jnp.where(strong, factor * drawn, drawn)


def block_scale(key, shape, shards, least, high):
    factor_of, own = 1.0, jax.random.fold_in(key, 6)
    for dim, shards_of in shards:
        heights = jnp.exp(jax.random.uniform(jax.random.fold_in(own, dim), (shards_of,), jnp.float32, least / len(shards), high / len(shards)))
        factor_of = factor_of * jnp.repeat(heights, shape[dim] // shards_of).reshape([-1 if axis == dim else 1 for axis in range(len(shape))])
    return factor_of


def bell_draw(rng, shape, deviation, reach, pieces=(), kind=jnp.bfloat16):
    drawn = deviation * jax.random.normal(rng, shape, jnp.float32)
    if pieces:
        drawn = drawn * block_scale(rng, shape, pieces, -0.22, 0.18)
    return jnp.clip(drawn, -reach, reach).astype(kind)


def heavy_noise(own_key, extent, scale, bound, cuts, heavy, held_as=jnp.bfloat16):
    drawn = scale * jax.random.normal(own_key, extent, jnp.float32)
    if cuts:
        drawn = drawn * block_scale(own_key, extent, cuts, -0.22, 0.18)
    return jnp.clip(with_spikes(drawn, jax.random.fold_in(own_key, 3), *heavy), -bound, bound).astype(held_as)


def setup_inputs(seed: int = 0, part: int = 0) -> dict:
    seeds = jax.random.split(jax.random.key(seed), 5)
    own_keys = jax.random.split(jax.random.fold_in(seeds[4], part), 5)
    return {
        "basis": heavy_noise(own_keys[0], (NROWS, BASIS), 1.0, 6.0, ((0, 16),), (0, 1, 16, 2.0)),
        "blocks": bell_draw(own_keys[1], (PARAMS, NROWB, SLOTS, BLOCK, BLOCK), (SLOTS * BLOCK * NROWS) ** -0.5, 0.0017089844, ((1, 16),)),
        "columns": plant(jax.random.randint(own_keys[2], (PARAMS, NROWB, SLOTS - 1), 0, ROWBLK + 2 * HALO), jax.random.fold_in(own_keys[2], 1), 0, (ROWBLK + 2 * HALO) - 1).astype(jnp.int32),
        "sends": plant(jax.random.randint(own_keys[3], (N_MESH, 2 * HALO), 0, ROWBLK), jax.random.fold_in(own_keys[3], 1), 0, ROWBLK - 1).astype(jnp.int32),
    }


def take_rows(source, positions):
    return jnp.take(source, positions, axis=0)


def reference(basis, blocks, columns, sends):
    own_blocks = basis.reshape(N_MESH, ROWBLK, BLOCK, BASIS)
    picker = jax.vmap(take_rows)
    upward = picker(own_blocks, sends[:, HALO:].astype(jnp.int32))
    downward = picker(own_blocks, sends[:, :HALO].astype(jnp.int32))
    empty_rim = jnp.zeros((1, HALO, BLOCK, BASIS), basis.dtype)
    from_below = jnp.concatenate([empty_rim, upward[:-1]], axis=0)
    from_above = jnp.concatenate([downward[1:], empty_rim], axis=0)
    extended = jnp.concatenate([own_blocks, from_below, from_above], axis=1)
    diag_index = jnp.broadcast_to(jnp.arange(ROWBLK, dtype=jnp.int32)[None, :, None], (N_MESH, ROWBLK, 1))

    def project_param(param):
        slot_index = jnp.concatenate([diag_index, columns[param].reshape(N_MESH, ROWBLK, SLOTS - 1).astype(jnp.int32)], axis=2)
        param_blocks = blocks[param].reshape(N_MESH, ROWBLK, SLOTS, BLOCK, BLOCK)
        accumulated = jnp.zeros((N_MESH, ROWBLK, BLOCK, BASIS), jnp.float32)
        for slot in range(SLOTS):
            gathered = picker(extended, slot_index[:, :, slot])
            accumulated = accumulated + jnp.einsum("dbik,dbkj->dbij", param_blocks[:, :, slot].astype(jnp.float32), gathered.astype(jnp.float32))
        image_rows = accumulated.astype(jnp.bfloat16).reshape(NROWS, BASIS)
        return lax.dot_general(basis, image_rows, (((0,), (0,)), ((), ())), preferred_element_type=jnp.float32)

    return jnp.concatenate([project_param(param) for param in range(PARAMS)], axis=1)
```

```python
import functools

import jax
import jax.numpy as jnp
from jax import lax
from jax.experimental import pallas as pl
from jax.experimental.pallas import tpu as pltpu
from jax.sharding import PartitionSpec as P

MESH = pl.DeviceIdType.MESH
CORES = 2
LANES = 128


def from_behind(value, axis, steps):
    count = lax.axis_size(axis)
    leading, last = (max(0, -steps), min(count, count - steps))
    return lax.ppermute(value, axis, [(source, source + steps) for source in range(leading, last)])


def plain_shards(basis, blocks, columns, sends):
    count_params, count_blocks, count_slots, block_size, _ = blocks.shape
    basis_width = basis.shape[1]
    halo_count = sends.shape[1] // 2
    own_blocks = basis.reshape(count_blocks, block_size, basis_width)
    diag_index = jnp.arange(count_blocks, dtype=jnp.int32)[:, None]
    images = []
    upward = jnp.take(own_blocks, sends[0, halo_count:], axis=0)
    downward = jnp.take(own_blocks, sends[0, :halo_count], axis=0)
    from_below = from_behind(upward, "mesh", 1)
    from_above = from_behind(downward, "mesh", -1)
    extended = jnp.concatenate([own_blocks, from_below, from_above], axis=0)
    for param in range(count_params):
        slot_index = jnp.concatenate([diag_index, columns[param]], axis=1)
        gathered = jnp.take(extended, slot_index, axis=0)
        accumulated = jnp.einsum(
            "bsik,bskj->bij", blocks[param], gathered, preferred_element_type=jnp.float32
        )
        images.append(
            accumulated.astype(jnp.bfloat16).reshape(count_blocks * block_size, basis_width)
        )
    stacked_images = jnp.concatenate(images, axis=1)
    return lax.psum_scatter(
        lax.dot_general(
            basis, stacked_images, (((0,), (0,)), ((), ())), preferred_element_type=jnp.float32
        ),
        "mesh",
        scatter_dimension=0,
        tiled=True,
    )


def chip_grid(chips):
    across = 1
    while (2 * across) ** 2 < chips and chips % (2 * across) == 0:
        across *= 2
    return chips // across, across


def kernel(n, zs, xs, width, basis, blocks, columns, sends, out, *scratch):
    chunks = basis.shape[2] // width
    own, scratch = scratch[:chunks], scratch[chunks:]
    ext, scratch = scratch[:chunks], scratch[chunks:]
    (
        stage, turned, ops, image, pair_out, pair_in, half_sum, z_out, z_in, x_sum, x_out, x_in,
        own_sem, ext_sem, ops_sem, halo_send, halo_recv,
        pair_send, pair_recv, z_send, z_recv, x_send, x_recv,
    ) = scratch
    params, count, slots, size, _ = blocks.shape
    basis_width = basis.shape[2]
    rows = count * size
    halo = sends.shape[1] // 2
    half = basis_width // CORES
    each = basis_width // n
    z_rows = half // zs

    me = lax.axis_index("mesh")
    core = lax.rem(me, CORES)
    chip = me // CORES
    x = lax.rem(chip, xs)
    z = chip // xs
    partner = me + 1 - 2 * core
    outer = me - 1 + 2 * core
    has_outer = jnp.logical_and(outer >= 0, outer < n)

    def at_z(step):
        return (lax.rem(z + step, zs) * xs + x) * CORES + core

    def at_x(step):
        return (z * xs + lax.rem(x + step, xs)) * CORES + core

    def own_copy(k):
        return pltpu.make_async_copy(
            basis.at[:, :, pl.ds(k * width, width)], own[k], own_sem.at[k]
        )

    def ext_copy(k):
        return pltpu.make_async_copy(
            basis.at[:, :, pl.ds(k * width, width)], ext[k].at[pl.ds(0, count)], ext_sem.at[k]
        )

    ops_copy = pltpu.make_async_copy(blocks, ops, ops_sem)

    def halo_copy(k, way):
        return pltpu.make_async_remote_copy(
            src_ref=stage.at[k, way],
            dst_ref=ext[k].at[pl.ds(count + way * halo, halo)],
            send_sem=halo_send.at[k, way],
            recv_sem=halo_recv.at[k, way],
            device_id={"mesh": me + 1 - 2 * way},
            device_id_type=MESH,
        )

    def pair_copy(k):
        return pltpu.make_async_remote_copy(
            src_ref=pair_out.at[k], dst_ref=pair_in.at[k],
            send_sem=pair_send.at[k], recv_sem=pair_recv.at[k],
            device_id={"mesh": partner}, device_id_type=MESH,
        )

    def z_copy(k, step):
        target = lax.rem(z + step, zs)
        return pltpu.make_async_remote_copy(
            src_ref=z_out.at[k, target], dst_ref=z_in.at[k, step - 1],
            send_sem=z_send.at[k, step - 1], recv_sem=z_recv.at[k, step - 1],
            device_id={"mesh": at_z(step)}, device_id_type=MESH,
        )

    def x_copy(k, step):
        target = lax.rem(x + step, xs)
        return pltpu.make_async_remote_copy(
            src_ref=x_out.at[k, target], dst_ref=x_in.at[k, step - 1],
            send_sem=x_send.at[k, step - 1], recv_sem=x_recv.at[k, step - 1],
            device_id={"mesh": at_x(step)}, device_id_type=MESH,
        )

    has = (me < n - 1, me > 0)
    gets = (me > 0, me < n - 1)

    for k in range(chunks):
        own_copy(k).start()
    barrier = pltpu.get_barrier_semaphore()
    peers = [partner] + [at_z(s) for s in range(1, zs)] + [at_x(s) for s in range(1, xs)]
    for peer in peers:
        pl.semaphore_signal(barrier, inc=1, device_id={"mesh": peer}, device_id_type=MESH)

    @pl.when(has_outer)
    def _():
        pl.semaphore_signal(barrier, inc=1, device_id={"mesh": outer}, device_id_type=MESH)

    for k in range(chunks):
        ext_copy(k).start()
    ops_copy.start()

    for k in range(chunks):
        own_copy(k).wait()
        for way, first in ((0, halo), (1, 0)):
            for h in range(halo):
                stage[k, way, h] = own[k][sends[0, first + h]]
        if k == 0:
            pl.semaphore_wait(barrier, len(peers) + has_outer.astype(jnp.int32))

        for way in range(2):
            @pl.when(has[way])
            def _():
                halo_copy(k, way).start()

    for way in range(2):
        @pl.when(jnp.logical_not(gets[way]))
        def _():
            for k in range(chunks):
                ext[k][pl.ds(count + way * halo, halo)] = jnp.zeros(
                    (halo, size, width), jnp.bfloat16
                )

    per_chunk = width // each
    pair_rows = 2 * size
    for k in range(chunks):
        def turn(r, carry):
            start = pl.multiple_of(r * pair_rows, pair_rows)
            flipped = own[k][pl.ds(r * 2, 2)].reshape(pair_rows, width).T
            for q in range(per_chunk):
                d = k * per_chunk + q
                place = (d % CORES) * half + (d // CORES) * each
                turned[place:place + each, pl.ds(start, pair_rows)] = flipped[
                    q * each:(q + 1) * each
                ]
            return carry

        lax.fori_loop(0, count // 2, turn, 0)

    ops_copy.wait()
    for k in range(chunks):
        ext_copy(k).wait()

    def z_send_all(k):
        pair_copy(k).wait_recv()
        total = half_sum[k] + pair_in[k].reshape(zs, z_rows, params * width).astype(jnp.float32)
        half_sum[k] = total
        z_out[k] = total.astype(jnp.bfloat16)
        for s in range(1, zs):
            z_copy(k, s).start()

    def x_send_all(k):
        total = half_sum[k, z]
        for s in range(1, zs):
            z_copy(k, s).wait_recv()
            total = total + z_in[k, s - 1].astype(jnp.float32)
        total = total.reshape(xs, each, params * width)
        x_sum[k] = total
        x_out[k] = total.astype(jnp.bfloat16)
        for s in range(1, xs):
            x_copy(k, s).start()

    def finish(k):
        total = x_sum[k, x]
        for s in range(1, xs):
            x_copy(k, s).wait_recv()
            total = total + x_in[k, s - 1].astype(jnp.float32)
        for p in range(params):
            out[:, p * basis_width + k * width:p * basis_width + (k + 1) * width] = total[
                :, p * width:(p + 1) * width
            ]

    for k in range(chunks):
        for way in range(2):
            @pl.when(gets[way])
            def _():
                halo_copy(k, way).wait_recv()

        def apply(g, carry):
            row = pl.multiple_of(g * size, size)
            diag = ext[k][g]
            for p in range(params):
                parts = [diag]
                for s in range(1, slots):
                    parts.append(ext[k][columns[p, s - 1, g]])
                left = jnp.concatenate([ops[p, g, s] for s in range(slots)], axis=1)
                made = jnp.dot(
                    left, jnp.concatenate(parts, axis=0), preferred_element_type=jnp.float32
                )
                image[pl.ds(row, size), p * width:(p + 1) * width] = made.astype(jnp.bfloat16)
            return carry

        lax.fori_loop(0, count, apply, 0, unroll=4)

        theirs = pl.multiple_of((1 - core) * half, half)
        pair_out[k] = jnp.dot(
            turned[pl.ds(theirs, half), :], image[...], preferred_element_type=jnp.float32
        ).astype(jnp.bfloat16)
        pair_copy(k).start()
        mine = pl.multiple_of(core * half, half)
        half_sum[k] = jnp.dot(
            turned[pl.ds(mine, half), :], image[...], preferred_element_type=jnp.float32
        ).reshape(zs, z_rows, params * width)
        if k > 0:
            x_send_all(k - 1)
        z_send_all(k)
        if k > 0:
            finish(k - 1)
    x_send_all(chunks - 1)
    finish(chunks - 1)

    for k in range(chunks):
        for way in range(2):
            @pl.when(has[way])
            def _():
                halo_copy(k, way).wait_send()
        pair_copy(k).wait_send()
        for s in range(1, zs):
            z_copy(k, s).wait_send()
        for s in range(1, xs):
            x_copy(k, s).wait_send()


def fused_shards(n, basis, blocks, columns, sends):
    params, count, slots, size, _ = blocks.shape
    rows, basis_width = basis.shape
    halo = sends.shape[1] // 2
    zs, xs = chip_grid(n // CORES)
    width = LANES
    chunks = basis_width // width
    each, half = basis_width // n, basis_width // CORES
    bf, f32 = jnp.bfloat16, jnp.float32
    wide = params * width
    dma = pltpu.SemaphoreType.DMA
    return pl.pallas_call(
        functools.partial(kernel, n, zs, xs, width),
        out_shape=jax.ShapeDtypeStruct((each, params * basis_width), f32),
        in_specs=[
            pl.BlockSpec(memory_space=pl.ANY),
            pl.BlockSpec(memory_space=pl.ANY),
            pl.BlockSpec(memory_space=pltpu.SMEM),
            pl.BlockSpec(memory_space=pltpu.SMEM),
        ],
        out_specs=pl.BlockSpec(memory_space=pltpu.VMEM),
        scratch_shapes=[pltpu.VMEM((count, size, width), bf) for _ in range(chunks)]
        + [pltpu.VMEM((count + 2 * halo, size, width), bf) for _ in range(chunks)]
        + [
            pltpu.VMEM((chunks, 2, halo, size, width), bf),
            pltpu.VMEM((basis_width, rows), bf),
            pltpu.VMEM(blocks.shape, bf),
            pltpu.VMEM((rows, wide), bf),
            pltpu.VMEM((chunks, half, wide), bf),
            pltpu.VMEM((chunks, half, wide), bf),
            pltpu.VMEM((chunks, zs, half // zs, wide), f32),
            pltpu.VMEM((chunks, zs, half // zs, wide), bf),
            pltpu.VMEM((chunks, zs, half // zs, wide), bf),
            pltpu.VMEM((chunks, xs, each, wide), f32),
            pltpu.VMEM((chunks, xs, each, wide), bf),
            pltpu.VMEM((chunks, xs, each, wide), bf),
            dma((chunks,)),
            dma((chunks,)),
            dma,
            dma((chunks, 2)),
            dma((chunks, 2)),
            dma((chunks,)),
            dma((chunks,)),
            dma((chunks, zs)),
            dma((chunks, zs)),
            dma((chunks, xs)),
            dma((chunks, xs)),
        ],
        compiler_params=pltpu.CompilerParams(collective_id=0, has_side_effects=True),
    )(basis.reshape(count, size, basis_width), blocks, jnp.swapaxes(columns, 1, 2), sends)


def solution(mesh):
    n = mesh.shape["mesh"]

    def shards(basis, blocks, columns, sends):
        each = basis.shape[1] // n
        tiled = basis.shape[1] % (n * 16) == 0 and LANES % max(each, 1) == 0
        if n % CORES == 0 and tiled and blocks.shape[3] == LANES:
            return fused_shards(n, basis, blocks, columns, sends)
        return plain_shards(basis, blocks, columns, sends)

    placed = (
        P(("grp", "mesh"), None),
        P(None, ("grp", "mesh"), None, None, None),
        P(None, ("grp", "mesh"), None),
        P(("grp", "mesh"), None),
    )
    return jax.shard_map(
        shards, mesh=mesh, in_specs=placed, out_specs=P(("grp", "mesh"), None), check_vma=False
    )
```

```python
import functools

import jax
import jax.numpy as jnp
from jax import lax
from jax.experimental import pallas as pl
from jax.experimental.pallas import tpu as pltpu
from jax.sharding import PartitionSpec as P

MESH = pl.DeviceIdType.MESH
CORES = 2
LANES = 128
AHEAD = 2


def from_behind(value, axis, steps):
    count = lax.axis_size(axis)
    leading, last = (max(0, -steps), min(count, count - steps))
    return lax.ppermute(value, axis, [(source, source + steps) for source in range(leading, last)])


def plain_shards(basis, blocks, columns, sends):
    count_params, count_blocks, count_slots, block_size, _ = blocks.shape
    basis_width = basis.shape[1]
    halo_count = sends.shape[1] // 2
    own_blocks = basis.reshape(count_blocks, block_size, basis_width)
    diag_index = jnp.arange(count_blocks, dtype=jnp.int32)[:, None]
    images = []
    upward = jnp.take(own_blocks, sends[0, halo_count:], axis=0)
    downward = jnp.take(own_blocks, sends[0, :halo_count], axis=0)
    from_below = from_behind(upward, "mesh", 1)
    from_above = from_behind(downward, "mesh", -1)
    extended = jnp.concatenate([own_blocks, from_below, from_above], axis=0)
    for param in range(count_params):
        slot_index = jnp.concatenate([diag_index, columns[param]], axis=1)
        gathered = jnp.take(extended, slot_index, axis=0)
        accumulated = jnp.einsum(
            "bsik,bskj->bij", blocks[param], gathered, preferred_element_type=jnp.float32
        )
        images.append(
            accumulated.astype(jnp.bfloat16).reshape(count_blocks * block_size, basis_width)
        )
    stacked_images = jnp.concatenate(images, axis=1)
    return lax.psum_scatter(
        lax.dot_general(
            basis, stacked_images, (((0,), (0,)), ((), ())), preferred_element_type=jnp.float32
        ),
        "mesh",
        scatter_dimension=0,
        tiled=True,
    )


def chip_grid(chips):
    across = 1
    while (2 * across) ** 2 < chips and chips % (2 * across) == 0:
        across *= 2
    return chips // across, across


def kernel(n, zs, xs, width, basis, blocks, columns, sends, out, *scratch):
    chunks = basis.shape[2] // width
    own, scratch = scratch[:chunks], scratch[chunks:]
    ext, scratch = scratch[:chunks], scratch[chunks:]
    (
        stage, turned, ops, image, pair_out, pair_in, half_sum, z_out, z_in, x_sum, x_out, x_in,
        own_sem, ext_sem, ops_sem, halo_send, halo_recv,
        pair_send, pair_recv, z_send, z_recv, x_send, x_recv,
    ) = scratch
    params, count, slots, size, _ = blocks.shape
    basis_width = basis.shape[2]
    rows = count * size
    halo = sends.shape[1] // 2
    half = basis_width // CORES
    each = basis_width // n
    z_rows = half // zs

    me = lax.axis_index("mesh")
    core = lax.rem(me, CORES)
    chip = me // CORES
    x = lax.rem(chip, xs)
    z = chip // xs
    partner = me + 1 - 2 * core
    outer = me - 1 + 2 * core
    has_outer = jnp.logical_and(outer >= 0, outer < n)

    def at_z(step):
        return (lax.rem(z + step, zs) * xs + x) * CORES + core

    def at_x(step):
        return (z * xs + lax.rem(x + step, xs)) * CORES + core

    def own_copy(k):
        return pltpu.make_async_copy(
            basis.at[:, :, pl.ds(k * width, width)], own[k], own_sem.at[k]
        )

    def ext_copy(k):
        return pltpu.make_async_copy(
            basis.at[:, :, pl.ds(k * width, width)], ext[k].at[pl.ds(0, count)], ext_sem.at[k]
        )

    ops_copy = pltpu.make_async_copy(blocks, ops, ops_sem)

    def halo_copy(k, way):
        return pltpu.make_async_remote_copy(
            src_ref=stage.at[k, way],
            dst_ref=ext[k].at[pl.ds(count + way * halo, halo)],
            send_sem=halo_send.at[k, way],
            recv_sem=halo_recv.at[k, way],
            device_id={"mesh": me + 1 - 2 * way},
            device_id_type=MESH,
        )

    def pair_copy(k):
        return pltpu.make_async_remote_copy(
            src_ref=pair_out.at[k], dst_ref=pair_in.at[k],
            send_sem=pair_send.at[k], recv_sem=pair_recv.at[k],
            device_id={"mesh": partner}, device_id_type=MESH,
        )

    def z_copy(k, step):
        target = lax.rem(z + step, zs)
        return pltpu.make_async_remote_copy(
            src_ref=z_out.at[k, target], dst_ref=z_in.at[k, step - 1],
            send_sem=z_send.at[k, step - 1], recv_sem=z_recv.at[k, step - 1],
            device_id={"mesh": at_z(step)}, device_id_type=MESH,
        )

    def x_copy(k, step):
        target = lax.rem(x + step, xs)
        return pltpu.make_async_remote_copy(
            src_ref=x_out.at[k, target], dst_ref=x_in.at[k, step - 1],
            send_sem=x_send.at[k, step - 1], recv_sem=x_recv.at[k, step - 1],
            device_id={"mesh": at_x(step)}, device_id_type=MESH,
        )

    has = (me < n - 1, me > 0)
    gets = (me > 0, me < n - 1)

    def halo_start(k):
        for way in range(2):
            @pl.when(has[way])
            def _():
                halo_copy(k, way).start()

    for k in range(chunks):
        own_copy(k).start()
    barrier = pltpu.get_barrier_semaphore()
    peers = [partner] + [at_z(s) for s in range(1, zs)] + [at_x(s) for s in range(1, xs)]
    for peer in peers:
        pl.semaphore_signal(barrier, inc=1, device_id={"mesh": peer}, device_id_type=MESH)

    @pl.when(has_outer)
    def _():
        pl.semaphore_signal(barrier, inc=1, device_id={"mesh": outer}, device_id_type=MESH)

    for k in range(chunks):
        ext_copy(k).start()
    ops_copy.start()

    for k in range(chunks):
        own_copy(k).wait()
        for way, first in ((0, halo), (1, 0)):
            for h in range(halo):
                stage[k, way, h] = own[k][sends[0, first + h]]
        if k == 0:
            pl.semaphore_wait(barrier, len(peers) + has_outer.astype(jnp.int32))

        if k < AHEAD:
            halo_start(k)

    for way in range(2):
        @pl.when(jnp.logical_not(gets[way]))
        def _():
            for k in range(chunks):
                ext[k][pl.ds(count + way * halo, halo)] = jnp.zeros(
                    (halo, size, width), jnp.bfloat16
                )

    per_chunk = width // each
    pair_rows = 2 * size
    for k in range(chunks):
        def turn(r, carry):
            start = pl.multiple_of(r * pair_rows, pair_rows)
            flipped = own[k][pl.ds(r * 2, 2)].reshape(pair_rows, width).T
            for q in range(per_chunk):
                d = k * per_chunk + q
                place = (d % CORES) * half + (d // CORES) * each
                turned[place:place + each, pl.ds(start, pair_rows)] = flipped[
                    q * each:(q + 1) * each
                ]
            return carry

        lax.fori_loop(0, count // 2, turn, 0)

    ops_copy.wait()
    for k in range(chunks):
        ext_copy(k).wait()

    def z_send_all(k):
        pair_copy(k).wait_recv()
        total = half_sum[k] + pair_in[k].reshape(zs, z_rows, params * width).astype(jnp.float32)
        half_sum[k] = total
        z_out[k] = total.astype(jnp.bfloat16)
        for s in range(1, zs):
            z_copy(k, s).start()

    def x_send_all(k):
        total = half_sum[k, z]
        for s in range(1, zs):
            z_copy(k, s).wait_recv()
            total = total + z_in[k, s - 1].astype(jnp.float32)
        total = total.reshape(xs, each, params * width)
        x_sum[k] = total
        x_out[k] = total.astype(jnp.bfloat16)
        for s in range(1, xs):
            x_copy(k, s).start()

    def finish(k):
        total = x_sum[k, x]
        for s in range(1, xs):
            x_copy(k, s).wait_recv()
            total = total + x_in[k, s - 1].astype(jnp.float32)
        for p in range(params):
            out[:, p * basis_width + k * width:p * basis_width + (k + 1) * width] = total[
                :, p * width:(p + 1) * width
            ]

    for k in range(chunks):
        for way in range(2):
            @pl.when(gets[way])
            def _():
                halo_copy(k, way).wait_recv()

        def apply(g, carry):
            row = pl.multiple_of(g * size, size)
            diag = ext[k][g]
            for p in range(params):
                parts = [diag]
                for s in range(1, slots):
                    parts.append(ext[k][columns[p, s - 1, g]])
                left = jnp.concatenate([ops[p, g, s] for s in range(slots)], axis=1)
                made = jnp.dot(
                    left, jnp.concatenate(parts, axis=0), preferred_element_type=jnp.float32
                )
                image[pl.ds(row, size), p * width:(p + 1) * width] = made.astype(jnp.bfloat16)
            return carry

        lax.fori_loop(0, count, apply, 0, unroll=4)

        theirs = pl.multiple_of((1 - core) * half, half)
        pair_out[k] = jnp.dot(
            turned[pl.ds(theirs, half), :], image[...], preferred_element_type=jnp.float32
        ).astype(jnp.bfloat16)
        pair_copy(k).start()
        mine = pl.multiple_of(core * half, half)
        half_sum[k] = jnp.dot(
            turned[pl.ds(mine, half), :], image[...], preferred_element_type=jnp.float32
        ).reshape(zs, z_rows, params * width)
        z_send_all(k)
        if k + AHEAD < chunks:
            halo_start(k + AHEAD)
    for k in range(chunks):
        x_send_all(k)
    for k in range(chunks):
        finish(k)

    for k in range(chunks):
        for way in range(2):
            @pl.when(has[way])
            def _():
                halo_copy(k, way).wait_send()
        pair_copy(k).wait_send()
        for s in range(1, zs):
            z_copy(k, s).wait_send()
        for s in range(1, xs):
            x_copy(k, s).wait_send()


def fused_shards(n, basis, blocks, columns, sends):
    params, count, slots, size, _ = blocks.shape
    rows, basis_width = basis.shape
    halo = sends.shape[1] // 2
    zs, xs = chip_grid(n // CORES)
    width = LANES
    chunks = basis_width // width
    each, half = basis_width // n, basis_width // CORES
    bf, f32 = jnp.bfloat16, jnp.float32
    wide = params * width
    dma = pltpu.SemaphoreType.DMA
    return pl.pallas_call(
        functools.partial(kernel, n, zs, xs, width),
        out_shape=jax.ShapeDtypeStruct((each, params * basis_width), f32),
        in_specs=[
            pl.BlockSpec(memory_space=pl.ANY),
            pl.BlockSpec(memory_space=pl.ANY),
            pl.BlockSpec(memory_space=pltpu.SMEM),
            pl.BlockSpec(memory_space=pltpu.SMEM),
        ],
        out_specs=pl.BlockSpec(memory_space=pltpu.VMEM),
        scratch_shapes=[pltpu.VMEM((count, size, width), bf) for _ in range(chunks)]
        + [pltpu.VMEM((count + 2 * halo, size, width), bf) for _ in range(chunks)]
        + [
            pltpu.VMEM((chunks, 2, halo, size, width), bf),
            pltpu.VMEM((basis_width, rows), bf),
            pltpu.VMEM(blocks.shape, bf),
            pltpu.VMEM((rows, wide), bf),
            pltpu.VMEM((chunks, half, wide), bf),
            pltpu.VMEM((chunks, half, wide), bf),
            pltpu.VMEM((chunks, zs, half // zs, wide), f32),
            pltpu.VMEM((chunks, zs, half // zs, wide), bf),
            pltpu.VMEM((chunks, zs, half // zs, wide), bf),
            pltpu.VMEM((chunks, xs, each, wide), f32),
            pltpu.VMEM((chunks, xs, each, wide), bf),
            pltpu.VMEM((chunks, xs, each, wide), bf),
            dma((chunks,)),
            dma((chunks,)),
            dma,
            dma((chunks, 2)),
            dma((chunks, 2)),
            dma((chunks,)),
            dma((chunks,)),
            dma((chunks, zs)),
            dma((chunks, zs)),
            dma((chunks, xs)),
            dma((chunks, xs)),
        ],
        compiler_params=pltpu.CompilerParams(collective_id=0, has_side_effects=True),
    )(basis.reshape(count, size, basis_width), blocks, jnp.swapaxes(columns, 1, 2), sends)


def solution(mesh):
    n = mesh.shape["mesh"]

    def shards(basis, blocks, columns, sends):
        each = basis.shape[1] // n
        tiled = basis.shape[1] % (n * 16) == 0 and LANES % max(each, 1) == 0
        if n % CORES == 0 and tiled and blocks.shape[3] == LANES:
            return fused_shards(n, basis, blocks, columns, sends)
        return plain_shards(basis, blocks, columns, sends)

    placed = (
        P(("grp", "mesh"), None),
        P(None, ("grp", "mesh"), None, None, None),
        P(None, ("grp", "mesh"), None),
        P(("grp", "mesh"), None),
    )
    return jax.shard_map(
        shards, mesh=mesh, in_specs=placed, out_specs=P(("grp", "mesh"), None), check_vma=False
    )
```

```python
import functools

import jax
import jax.numpy as jnp
from jax import lax
from jax.experimental import pallas as pl
from jax.experimental.pallas import tpu as pltpu
from jax.sharding import PartitionSpec as P

MESH = pl.DeviceIdType.MESH
CORES = 2
LANES = 128
AHEAD = 2
FAR = 1


def from_behind(value, axis, steps):
    count = lax.axis_size(axis)
    leading, last = (max(0, -steps), min(count, count - steps))
    return lax.ppermute(value, axis, [(source, source + steps) for source in range(leading, last)])


def plain_shards(basis, blocks, columns, sends):
    count_params, count_blocks, count_slots, block_size, _ = blocks.shape
    basis_width = basis.shape[1]
    halo_count = sends.shape[1] // 2
    own_blocks = basis.reshape(count_blocks, block_size, basis_width)
    diag_index = jnp.arange(count_blocks, dtype=jnp.int32)[:, None]
    images = []
    upward = jnp.take(own_blocks, sends[0, halo_count:], axis=0)
    downward = jnp.take(own_blocks, sends[0, :halo_count], axis=0)
    from_below = from_behind(upward, "mesh", 1)
    from_above = from_behind(downward, "mesh", -1)
    extended = jnp.concatenate([own_blocks, from_below, from_above], axis=0)
    for param in range(count_params):
        slot_index = jnp.concatenate([diag_index, columns[param]], axis=1)
        gathered = jnp.take(extended, slot_index, axis=0)
        accumulated = jnp.einsum(
            "bsik,bskj->bij", blocks[param], gathered, preferred_element_type=jnp.float32
        )
        images.append(
            accumulated.astype(jnp.bfloat16).reshape(count_blocks * block_size, basis_width)
        )
    stacked_images = jnp.concatenate(images, axis=1)
    return lax.psum_scatter(
        lax.dot_general(
            basis, stacked_images, (((0,), (0,)), ((), ())), preferred_element_type=jnp.float32
        ),
        "mesh",
        scatter_dimension=0,
        tiled=True,
    )


def chip_grid(chips):
    across = 1
    while (2 * across) ** 2 < chips and chips % (2 * across) == 0:
        across *= 2
    return chips // across, across


def kernel(n, zs, xs, width, basis, blocks, columns, sends, out, *scratch):
    chunks = basis.shape[2] // width
    own, scratch = scratch[:chunks], scratch[chunks:]
    ext, scratch = scratch[:chunks], scratch[chunks:]
    (
        stage, turned, ops, image, pair_out, pair_in, half_sum, z_out, z_in, x_sum, x_out, x_in, far_in,
        own_sem, ext_sem, ops_sem, halo_send, halo_recv,
        pair_send, pair_recv, z_send, z_recv, x_send, x_recv, far_send, far_recv,
    ) = scratch
    params, count, slots, size, _ = blocks.shape
    basis_width = basis.shape[2]
    rows = count * size
    halo = sends.shape[1] // 2
    half = basis_width // CORES
    each = basis_width // n
    chips = zs * xs
    hops = chunks - FAR

    me = lax.axis_index("mesh")
    core = lax.rem(me, CORES)
    chip = me // CORES
    x = lax.rem(chip, xs)
    z = chip // xs
    partner = me + 1 - 2 * core
    outer = me - 1 + 2 * core
    has_outer = jnp.logical_and(outer >= 0, outer < n)

    def at_z(step):
        return (lax.rem(z + step, zs) * xs + x) * CORES + core

    def at_x(step):
        return (z * xs + lax.rem(x + step, xs)) * CORES + core

    def own_copy(k):
        return pltpu.make_async_copy(
            basis.at[:, :, pl.ds(k * width, width)], own[k], own_sem.at[k]
        )

    def ext_copy(k):
        return pltpu.make_async_copy(
            basis.at[:, :, pl.ds(k * width, width)], ext[k].at[pl.ds(0, count)], ext_sem.at[k]
        )

    ops_copy = pltpu.make_async_copy(blocks, ops, ops_sem)

    def halo_copy(k, way):
        return pltpu.make_async_remote_copy(
            src_ref=stage.at[k, way],
            dst_ref=ext[k].at[pl.ds(count + way * halo, halo)],
            send_sem=halo_send.at[k, way],
            recv_sem=halo_recv.at[k, way],
            device_id={"mesh": me + 1 - 2 * way},
            device_id_type=MESH,
        )

    def pair_copy(k):
        return pltpu.make_async_remote_copy(
            src_ref=pair_out.at[k], dst_ref=pair_in.at[k],
            send_sem=pair_send.at[k], recv_sem=pair_recv.at[k],
            device_id={"mesh": partner}, device_id_type=MESH,
        )

    def z_copy(k, step):
        target = lax.rem(z + step, zs)
        return pltpu.make_async_remote_copy(
            src_ref=z_out.at[k, pl.ds(target * xs, xs)], dst_ref=z_in.at[k, step - 1],
            send_sem=z_send.at[k, step - 1], recv_sem=z_recv.at[k, step - 1],
            device_id={"mesh": at_z(step)}, device_id_type=MESH,
        )

    def x_copy(k, step):
        target = lax.rem(x + step, xs)
        return pltpu.make_async_remote_copy(
            src_ref=x_out.at[k, target], dst_ref=x_in.at[k, step - 1],
            send_sem=x_send.at[k, step - 1], recv_sem=x_recv.at[k, step - 1],
            device_id={"mesh": at_x(step)}, device_id_type=MESH,
        )

    def far_copy(k, step):
        target = lax.rem(chip + step, chips)
        at = k - hops
        return pltpu.make_async_remote_copy(
            src_ref=z_out.at[k, target], dst_ref=far_in.at[at, step - 1],
            send_sem=far_send.at[at, step - 1], recv_sem=far_recv.at[at, step - 1],
            device_id={"mesh": target * CORES + core}, device_id_type=MESH,
        )

    has = (me < n - 1, me > 0)
    gets = (me > 0, me < n - 1)

    def halo_start(k):
        for way in range(2):
            @pl.when(has[way])
            def _():
                halo_copy(k, way).start()

    for k in range(chunks):
        own_copy(k).start()
    barrier = pltpu.get_barrier_semaphore()
    peers = [partner] + [lax.rem(chip + s, chips) * CORES + core for s in range(1, chips)]
    for peer in peers:
        pl.semaphore_signal(barrier, inc=1, device_id={"mesh": peer}, device_id_type=MESH)

    @pl.when(has_outer)
    def _():
        pl.semaphore_signal(barrier, inc=1, device_id={"mesh": outer}, device_id_type=MESH)

    for k in range(chunks):
        ext_copy(k).start()
    ops_copy.start()

    for k in range(chunks):
        own_copy(k).wait()
        for way, first in ((0, halo), (1, 0)):
            for h in range(halo):
                stage[k, way, h] = own[k][sends[0, first + h]]
        if k == 0:
            pl.semaphore_wait(barrier, len(peers) + has_outer.astype(jnp.int32))

        if k < AHEAD:
            halo_start(k)

    for way in range(2):
        @pl.when(jnp.logical_not(gets[way]))
        def _():
            for k in range(chunks):
                ext[k][pl.ds(count + way * halo, halo)] = jnp.zeros(
                    (halo, size, width), jnp.bfloat16
                )

    per_chunk = width // each
    pair_rows = 2 * size
    for k in range(chunks):
        def turn(r, carry):
            start = pl.multiple_of(r * pair_rows, pair_rows)
            flipped = own[k][pl.ds(r * 2, 2)].reshape(pair_rows, width).T
            for q in range(per_chunk):
                d = k * per_chunk + q
                place = (d % CORES) * half + (d // CORES) * each
                turned[place:place + each, pl.ds(start, pair_rows)] = flipped[
                    q * each:(q + 1) * each
                ]
            return carry

        lax.fori_loop(0, count // 2, turn, 0)

    ops_copy.wait()
    for k in range(chunks):
        ext_copy(k).wait()

    def z_send_all(k):
        pair_copy(k).wait_recv()
        total = half_sum[k] + pair_in[k].reshape(chips, each, params * width).astype(jnp.float32)
        half_sum[k] = total
        z_out[k] = total.astype(jnp.bfloat16)
        if k < hops:
            for s in range(1, zs):
                z_copy(k, s).start()
        else:
            for s in range(1, chips):
                far_copy(k, s).start()

    def x_send_all(k):
        total = half_sum[k, pl.ds(z * xs, xs)]
        for s in range(1, zs):
            z_copy(k, s).wait_recv()
            total = total + z_in[k, s - 1].astype(jnp.float32)
        x_sum[k] = total
        x_out[k] = total.astype(jnp.bfloat16)
        for s in range(1, xs):
            x_copy(k, s).start()

    def finish(k):
        if k < hops:
            total = x_sum[k, x]
            for s in range(1, xs):
                x_copy(k, s).wait_recv()
                total = total + x_in[k, s - 1].astype(jnp.float32)
        else:
            total = half_sum[k, chip]
            for s in range(1, chips):
                far_copy(k, s).wait_recv()
                total = total + far_in[k - hops, s - 1].astype(jnp.float32)
        for p in range(params):
            out[:, p * basis_width + k * width:p * basis_width + (k + 1) * width] = total[
                :, p * width:(p + 1) * width
            ]

    for k in range(chunks):
        for way in range(2):
            @pl.when(gets[way])
            def _():
                halo_copy(k, way).wait_recv()

        def apply(g, carry):
            row = pl.multiple_of(g * size, size)
            diag = ext[k][g]
            for p in range(params):
                parts = [diag]
                for s in range(1, slots):
                    parts.append(ext[k][columns[p, s - 1, g]])
                left = jnp.concatenate([ops[p, g, s] for s in range(slots)], axis=1)
                made = jnp.dot(
                    left, jnp.concatenate(parts, axis=0), preferred_element_type=jnp.float32
                )
                image[pl.ds(row, size), p * width:(p + 1) * width] = made.astype(jnp.bfloat16)
            return carry

        lax.fori_loop(0, count, apply, 0, unroll=True)

        theirs = pl.multiple_of((1 - core) * half, half)
        pair_out[k] = jnp.dot(
            turned[pl.ds(theirs, half), :], image[...], preferred_element_type=jnp.float32
        ).astype(jnp.bfloat16)
        pair_copy(k).start()
        mine = pl.multiple_of(core * half, half)
        half_sum[k] = jnp.dot(
            turned[pl.ds(mine, half), :], image[...], preferred_element_type=jnp.float32
        ).reshape(chips, each, params * width)
        if k + AHEAD < chunks:
            halo_start(k + AHEAD)
        z_send_all(k)
        if 0 < k <= hops:
            x_send_all(k - 1)
    if FAR == 0:
        x_send_all(chunks - 1)
    for k in range(chunks):
        finish(k)

    for k in range(chunks):
        for way in range(2):
            @pl.when(has[way])
            def _():
                halo_copy(k, way).wait_send()
        pair_copy(k).wait_send()
        if k < hops:
            for s in range(1, zs):
                z_copy(k, s).wait_send()
            for s in range(1, xs):
                x_copy(k, s).wait_send()
        else:
            for s in range(1, chips):
                far_copy(k, s).wait_send()


def fused_shards(n, basis, blocks, columns, sends):
    params, count, slots, size, _ = blocks.shape
    rows, basis_width = basis.shape
    halo = sends.shape[1] // 2
    zs, xs = chip_grid(n // CORES)
    width = LANES
    chunks = basis_width // width
    each, half = basis_width // n, basis_width // CORES
    bf, f32 = jnp.bfloat16, jnp.float32
    wide = params * width
    dma = pltpu.SemaphoreType.DMA
    return pl.pallas_call(
        functools.partial(kernel, n, zs, xs, width),
        out_shape=jax.ShapeDtypeStruct((each, params * basis_width), f32),
        in_specs=[
            pl.BlockSpec(memory_space=pl.ANY),
            pl.BlockSpec(memory_space=pl.ANY),
            pl.BlockSpec(memory_space=pltpu.SMEM),
            pl.BlockSpec(memory_space=pltpu.SMEM),
        ],
        out_specs=pl.BlockSpec(memory_space=pltpu.VMEM),
        scratch_shapes=[pltpu.VMEM((count, size, width), bf) for _ in range(chunks)]
        + [pltpu.VMEM((count + 2 * halo, size, width), bf) for _ in range(chunks)]
        + [
            pltpu.VMEM((chunks, 2, halo, size, width), bf),
            pltpu.VMEM((basis_width, rows), bf),
            pltpu.VMEM(blocks.shape, bf),
            pltpu.VMEM((rows, wide), bf),
            pltpu.VMEM((chunks, half, wide), bf),
            pltpu.VMEM((chunks, half, wide), bf),
            pltpu.VMEM((chunks, zs * xs, each, wide), f32),
            pltpu.VMEM((chunks, zs * xs, each, wide), bf),
            pltpu.VMEM((chunks, zs, xs, each, wide), bf),
            pltpu.VMEM((chunks, xs, each, wide), f32),
            pltpu.VMEM((chunks, xs, each, wide), bf),
            pltpu.VMEM((chunks, xs, each, wide), bf),
            pltpu.VMEM((max(FAR, 1), zs * xs, each, wide), bf),
            dma((chunks,)),
            dma((chunks,)),
            dma,
            dma((chunks, 2)),
            dma((chunks, 2)),
            dma((chunks,)),
            dma((chunks,)),
            dma((chunks, zs)),
            dma((chunks, zs)),
            dma((chunks, xs)),
            dma((chunks, xs)),
            dma((max(FAR, 1), zs * xs)),
            dma((max(FAR, 1), zs * xs)),
        ],
        compiler_params=pltpu.CompilerParams(collective_id=0, has_side_effects=True),
    )(basis.reshape(count, size, basis_width), blocks, jnp.swapaxes(columns, 1, 2), sends)


def solution(mesh):
    n = mesh.shape["mesh"]

    def shards(basis, blocks, columns, sends):
        each = basis.shape[1] // n
        tiled = basis.shape[1] % (n * 16) == 0 and LANES % max(each, 1) == 0
        if n % CORES == 0 and tiled and blocks.shape[3] == LANES:
            return fused_shards(n, basis, blocks, columns, sends)
        return plain_shards(basis, blocks, columns, sends)

    placed = (
        P(("grp", "mesh"), None),
        P(None, ("grp", "mesh"), None, None, None),
        P(None, ("grp", "mesh"), None),
        P(("grp", "mesh"), None),
    )
    return jax.shard_map(
        shards, mesh=mesh, in_specs=placed, out_specs=P(("grp", "mesh"), None), check_vma=False
    )
```

```python
import functools

import jax
import jax.numpy as jnp
from jax import lax
from jax.experimental import pallas as pl
from jax.experimental.pallas import tpu as pltpu
from jax.sharding import PartitionSpec as P

MESH = pl.DeviceIdType.MESH
CORES = 2
LANES = 128
AHEAD = 2
FAR = 1


def from_behind(value, axis, steps):
    count = lax.axis_size(axis)
    leading, last = (max(0, -steps), min(count, count - steps))
    return lax.ppermute(value, axis, [(source, source + steps) for source in range(leading, last)])


def plain_shards(basis, blocks, columns, sends):
    count_params, count_blocks, count_slots, block_size, _ = blocks.shape
    basis_width = basis.shape[1]
    halo_count = sends.shape[1] // 2
    own_blocks = basis.reshape(count_blocks, block_size, basis_width)
    diag_index = jnp.arange(count_blocks, dtype=jnp.int32)[:, None]
    images = []
    upward = jnp.take(own_blocks, sends[0, halo_count:], axis=0)
    downward = jnp.take(own_blocks, sends[0, :halo_count], axis=0)
    from_below = from_behind(upward, "mesh", 1)
    from_above = from_behind(downward, "mesh", -1)
    extended = jnp.concatenate([own_blocks, from_below, from_above], axis=0)
    for param in range(count_params):
        slot_index = jnp.concatenate([diag_index, columns[param]], axis=1)
        gathered = jnp.take(extended, slot_index, axis=0)
        accumulated = jnp.einsum(
            "bsik,bskj->bij", blocks[param], gathered, preferred_element_type=jnp.float32
        )
        images.append(
            accumulated.astype(jnp.bfloat16).reshape(count_blocks * block_size, basis_width)
        )
    stacked_images = jnp.concatenate(images, axis=1)
    return lax.psum_scatter(
        lax.dot_general(
            basis, stacked_images, (((0,), (0,)), ((), ())), preferred_element_type=jnp.float32
        ),
        "mesh",
        scatter_dimension=0,
        tiled=True,
    )


def chip_grid(chips):
    across = 1
    while (2 * across) ** 2 < chips and chips % (2 * across) == 0:
        across *= 2
    return chips // across, across


def kernel(n, zs, xs, width, basis, blocks, columns, sends, out, *scratch):
    chunks = basis.shape[2] // width
    own, scratch = scratch[:chunks], scratch[chunks:]
    ext, scratch = scratch[:chunks], scratch[chunks:]
    (
        stage, turned, ops, image, pair_out, pair_in, half_sum, z_out, z_in, x_sum, x_out, x_in, far_in,
        own_sem, ext_sem, ops_sem, halo_send, halo_recv,
        pair_send, pair_recv, z_send, z_recv, x_send, x_recv, far_send, far_recv,
    ) = scratch
    params, count, slots, size, _ = blocks.shape
    basis_width = basis.shape[2]
    rows = count * size
    halo = sends.shape[1] // 2
    half = basis_width // CORES
    each = basis_width // n
    chips = zs * xs
    hops = chunks - FAR

    me = lax.axis_index("mesh")
    core = lax.rem(me, CORES)
    chip = me // CORES
    x = lax.rem(chip, xs)
    z = chip // xs
    partner = me + 1 - 2 * core
    outer = me - 1 + 2 * core
    has_outer = jnp.logical_and(outer >= 0, outer < n)

    def at_z(step):
        return (lax.rem(z + step, zs) * xs + x) * CORES + core

    def at_x(step):
        return (z * xs + lax.rem(x + step, xs)) * CORES + core

    def own_copy(k):
        return pltpu.make_async_copy(
            basis.at[:, :, pl.ds(k * width, width)], own[k], own_sem.at[k]
        )

    def ext_copy(k):
        return pltpu.make_async_copy(
            basis.at[:, :, pl.ds(k * width, width)], ext[k].at[pl.ds(0, count)], ext_sem.at[k]
        )

    ops_copy = pltpu.make_async_copy(blocks, ops, ops_sem)

    def halo_copy(k, way):
        return pltpu.make_async_remote_copy(
            src_ref=stage.at[k, way],
            dst_ref=ext[k].at[pl.ds(count + way * halo, halo)],
            send_sem=halo_send.at[k, way],
            recv_sem=halo_recv.at[k, way],
            device_id={"mesh": me + 1 - 2 * way},
            device_id_type=MESH,
        )

    def pair_copy(k):
        return pltpu.make_async_remote_copy(
            src_ref=pair_out.at[k], dst_ref=pair_in.at[k],
            send_sem=pair_send.at[k], recv_sem=pair_recv.at[k],
            device_id={"mesh": partner}, device_id_type=MESH,
        )

    def z_copy(k, step):
        target = lax.rem(z + step, zs)
        return pltpu.make_async_remote_copy(
            src_ref=z_out.at[k, pl.ds(target * xs, xs)], dst_ref=z_in.at[k, step - 1],
            send_sem=z_send.at[k, step - 1], recv_sem=z_recv.at[k, step - 1],
            device_id={"mesh": at_z(step)}, device_id_type=MESH,
        )

    def x_copy(k, step):
        target = lax.rem(x + step, xs)
        return pltpu.make_async_remote_copy(
            src_ref=x_out.at[k, target], dst_ref=x_in.at[k, step - 1],
            send_sem=x_send.at[k, step - 1], recv_sem=x_recv.at[k, step - 1],
            device_id={"mesh": at_x(step)}, device_id_type=MESH,
        )

    def far_copy(k, step):
        target = lax.rem(chip + step, chips)
        at = k - hops
        return pltpu.make_async_remote_copy(
            src_ref=z_out.at[k, target], dst_ref=far_in.at[at, step - 1],
            send_sem=far_send.at[at, step - 1], recv_sem=far_recv.at[at, step - 1],
            device_id={"mesh": target * CORES + core}, device_id_type=MESH,
        )

    has = (me < n - 1, me > 0)
    gets = (me > 0, me < n - 1)

    def halo_start(k):
        for way in range(2):
            @pl.when(has[way])
            def _():
                halo_copy(k, way).start()

    for k in range(chunks):
        own_copy(k).start()
    barrier = pltpu.get_barrier_semaphore()
    peers = [partner] + [lax.rem(chip + s, chips) * CORES + core for s in range(1, chips)]
    for peer in peers:
        pl.semaphore_signal(barrier, inc=1, device_id={"mesh": peer}, device_id_type=MESH)

    @pl.when(has_outer)
    def _():
        pl.semaphore_signal(barrier, inc=1, device_id={"mesh": outer}, device_id_type=MESH)

    for k in range(chunks):
        ext_copy(k).start()
    ops_copy.start()

    for k in range(chunks):
        own_copy(k).wait()
        for way, first in ((0, halo), (1, 0)):
            for h in range(halo):
                stage[k, way, h] = own[k][sends[0, first + h]]
        if k == 0:
            pl.semaphore_wait(barrier, len(peers) + has_outer.astype(jnp.int32))

        if k < AHEAD:
            halo_start(k)

    for way in range(2):
        @pl.when(jnp.logical_not(gets[way]))
        def _():
            for k in range(chunks):
                ext[k][pl.ds(count + way * halo, halo)] = jnp.zeros(
                    (halo, size, width), jnp.bfloat16
                )

    per_chunk = width // each
    pair_rows = 2 * size
    for k in range(chunks):
        def turn(r, carry):
            start = pl.multiple_of(r * pair_rows, pair_rows)
            flipped = own[k][pl.ds(r * 2, 2)].reshape(pair_rows, width).T
            for q in range(per_chunk):
                d = k * per_chunk + q
                place = (d % CORES) * half + (d // CORES) * each
                turned[place:place + each, pl.ds(start, pair_rows)] = flipped[
                    q * each:(q + 1) * each
                ]
            return carry

        lax.fori_loop(0, count // 2, turn, 0)

    ops_copy.wait()
    for k in range(chunks):
        ext_copy(k).wait()

    def z_send_all(k):
        pair_copy(k).wait_recv()
        total = half_sum[k] + pair_in[k].reshape(chips, each, params * width).astype(jnp.float32)
        half_sum[k] = total
        z_out[k] = total.astype(jnp.bfloat16)
        if k < hops:
            for s in range(1, zs):
                z_copy(k, s).start()
        else:
            for s in range(1, chips):
                far_copy(k, s).start()

    def x_send_all(k):
        total = half_sum[k, pl.ds(z * xs, xs)]
        for s in range(1, zs):
            z_copy(k, s).wait_recv()
            total = total + z_in[k, s - 1].astype(jnp.float32)
        x_sum[k] = total
        x_out[k] = total.astype(jnp.bfloat16)
        for s in range(1, xs):
            x_copy(k, s).start()

    def finish(k):
        if k < hops:
            total = x_sum[k, x]
            for s in range(1, xs):
                x_copy(k, s).wait_recv()
                total = total + x_in[k, s - 1].astype(jnp.float32)
        else:
            total = half_sum[k, chip]
            for s in range(1, chips):
                far_copy(k, s).wait_recv()
                total = total + far_in[k - hops, s - 1].astype(jnp.float32)
        for p in range(params):
            out[:, p * basis_width + k * width:p * basis_width + (k + 1) * width] = total[
                :, p * width:(p + 1) * width
            ]

    for k in range(chunks):
        for way in range(2):
            @pl.when(gets[way])
            def _():
                halo_copy(k, way).wait_recv()

        def apply(g, carry):
            row = pl.multiple_of(g * size, size)
            diag = ext[k][g]
            for p in range(params):
                parts = [diag]
                for s in range(1, slots):
                    parts.append(ext[k][columns[p, s - 1, g]])
                left = jnp.concatenate([ops[p, g, s] for s in range(slots)], axis=1)
                made = jnp.dot(
                    left, jnp.concatenate(parts, axis=0), preferred_element_type=jnp.float32
                )
                image[pl.ds(row, size), p * width:(p + 1) * width] = made.astype(jnp.bfloat16)
            return carry

        lax.fori_loop(0, count, apply, 0, unroll=count)

        theirs = pl.multiple_of((1 - core) * half, half)
        pair_out[k] = jnp.dot(
            turned[pl.ds(theirs, half), :], image[...], preferred_element_type=jnp.float32
        ).astype(jnp.bfloat16)
        pair_copy(k).start()
        mine = pl.multiple_of(core * half, half)
        half_sum[k] = jnp.dot(
            turned[pl.ds(mine, half), :], image[...], preferred_element_type=jnp.float32
        ).reshape(chips, each, params * width)
        z_send_all(k)
        if k + AHEAD < chunks:
            halo_start(k + AHEAD)
        if 0 < k <= hops:
            x_send_all(k - 1)
    if FAR == 0:
        x_send_all(chunks - 1)
    for k in range(chunks):
        finish(k)

    for k in range(chunks):
        for way in range(2):
            @pl.when(has[way])
            def _():
                halo_copy(k, way).wait_send()
        pair_copy(k).wait_send()
        if k < hops:
            for s in range(1, zs):
                z_copy(k, s).wait_send()
            for s in range(1, xs):
                x_copy(k, s).wait_send()
        else:
            for s in range(1, chips):
                far_copy(k, s).wait_send()


def fused_shards(n, basis, blocks, columns, sends):
    params, count, slots, size, _ = blocks.shape
    rows, basis_width = basis.shape
    halo = sends.shape[1] // 2
    zs, xs = chip_grid(n // CORES)
    width = LANES
    chunks = basis_width // width
    each, half = basis_width // n, basis_width // CORES
    bf, f32 = jnp.bfloat16, jnp.float32
    wide = params * width
    dma = pltpu.SemaphoreType.DMA
    return pl.pallas_call(
        functools.partial(kernel, n, zs, xs, width),
        out_shape=jax.ShapeDtypeStruct((each, params * basis_width), f32),
        in_specs=[
            pl.BlockSpec(memory_space=pl.ANY),
            pl.BlockSpec(memory_space=pl.ANY),
            pl.BlockSpec(memory_space=pltpu.SMEM),
            pl.BlockSpec(memory_space=pltpu.SMEM),
        ],
        out_specs=pl.BlockSpec(memory_space=pltpu.VMEM),
        scratch_shapes=[pltpu.VMEM((count, size, width), bf) for _ in range(chunks)]
        + [pltpu.VMEM((count + 2 * halo, size, width), bf) for _ in range(chunks)]
        + [
            pltpu.VMEM((chunks, 2, halo, size, width), bf),
            pltpu.VMEM((basis_width, rows), bf),
            pltpu.VMEM(blocks.shape, bf),
            pltpu.VMEM((rows, wide), bf),
            pltpu.VMEM((chunks, half, wide), bf),
            pltpu.VMEM((chunks, half, wide), bf),
            pltpu.VMEM((chunks, zs * xs, each, wide), f32),
            pltpu.VMEM((chunks, zs * xs, each, wide), bf),
            pltpu.VMEM((chunks, zs, xs, each, wide), bf),
            pltpu.VMEM((chunks, xs, each, wide), f32),
            pltpu.VMEM((chunks, xs, each, wide), bf),
            pltpu.VMEM((chunks, xs, each, wide), bf),
            pltpu.VMEM((max(FAR, 1), zs * xs, each, wide), bf),
            dma((chunks,)),
            dma((chunks,)),
            dma,
            dma((chunks, 2)),
            dma((chunks, 2)),
            dma((chunks,)),
            dma((chunks,)),
            dma((chunks, zs)),
            dma((chunks, zs)),
            dma((chunks, xs)),
            dma((chunks, xs)),
            dma((max(FAR, 1), zs * xs)),
            dma((max(FAR, 1), zs * xs)),
        ],
        compiler_params=pltpu.CompilerParams(collective_id=0, has_side_effects=True),
    )(basis.reshape(count, size, basis_width), blocks, jnp.swapaxes(columns, 1, 2), sends)


def solution(mesh):
    n = mesh.shape["mesh"]

    def shards(basis, blocks, columns, sends):
        each = basis.shape[1] // n
        tiled = basis.shape[1] % (n * 16) == 0 and LANES % max(each, 1) == 0
        if n % CORES == 0 and tiled and blocks.shape[3] == LANES:
            return fused_shards(n, basis, blocks, columns, sends)
        return plain_shards(basis, blocks, columns, sends)

    placed = (
        P(("grp", "mesh"), None),
        P(None, ("grp", "mesh"), None, None, None),
        P(None, ("grp", "mesh"), None),
        P(("grp", "mesh"), None),
    )
    return jax.shard_map(
        shards, mesh=mesh, in_specs=placed, out_specs=P(("grp", "mesh"), None), check_vma=False
    )
```
